1024 devices in a mesh: dp: 128 (over x, y, core), mp: 8 (over z).
Axes of the slice: x: 8, y: 8, z: 8, core: 2. Of those that a mesh axis runs over, the one named last changes fastest.
Arguments:
- inputs: bfloat16 [256, 256, 768], P('dp'), may hold values from -6 to 6
- cotangent: bfloat16 [256, 256, 768], P('dp'), may hold values from -24 to 24
- lengths: int32 [256], P('dp'), may hold values from 32 to 256, as said below
- kernel: float32 [31, 768], replicated, may hold values from -1 to 1
- norm_gain: float32 [768], replicated, may hold values from 0.1 to 1.9
- layer_scale: float32 [768], replicated, may hold values from 0.3 to 1.5
- w_in: bfloat16 [768, 3072], P('dp', 'mp'), may hold values from -0.21875 to 0.21875
- w_out: bfloat16 [3072, 768], P('mp', 'dp'), may hold values from -0.109375 to 0.109375
Outputs:
- output: bfloat16 [256, 256, 768], P('dp', 'mp')
- input_grad: bfloat16 [256, 256, 768], P('dp')
- grad_in: float32 [768, 3072], P('dp', 'mp')
- grad_out: float32 [3072, 768], P('mp', 'dp')
- grad_kernel: float32 [31, 768], P(None, 'dp')
- grad_gain: float32 [768], P('dp')
- grad_scale: float32 [768], P('dp')
The draws below stay inside these ranges and needn't reach their ends.
Inputs may be any that keep to these rules, and one draw needn't show every extreme that they name: `lengths`: valid tokens of each spectrum; in every draw some spectrum uses all 256 slots.
All inputs are finite; a program needn't handle non-finite values.
Results may differ from the reference program's by a relative error of at most 0.019.
Values may be sent and summed in bfloat16 or wider, within the bound.
No kernel may reach another device: no remote copies, remote signals or barrier semaphores. Data moves between devices by JAX's collectives and lax.ppermute only.
A program may use at most 64 MiB of HBM per device.

```python
import math
import jax
import jax.numpy as jnp
from jax import lax

D = 768
FF = 3072
KSIZE = 31
SEQ = 256
BATCH = 256
N_MP = 8


def draw_lengths(key, part):
    key_vals, key_pick = jax.random.split(jax.random.fold_in(key, 17))
    spectra = jnp.arange(BATCH, dtype=jnp.int32)
    lowest = SEQ // 8
    highest = lowest + (spectra + 1) * (SEQ - lowest) // BATCH + 1
    raw_bits = jax.random.randint(key_vals, (BATCH,), 0, 1 << 30, dtype=jnp.int32)
    values = lowest + raw_bits % (highest - lowest)
    chosen = jax.random.randint(key_pick, (), 0, BATCH, dtype=jnp.int32)
    return jnp.where(spectra == chosen, SEQ, values).astype(jnp.int32)


def raised(values, stream_key, source, target, parts, factor):
    owner, partner = [(jnp.arange(values.shape[axis_at]) // (values.shape[axis_at] // parts)).reshape([-1 if axis == axis_at else 1 for axis in range(values.ndim)]) for axis_at in (source, target)]
    chosen = jax.random.permutation(stream_key, parts)[partner]
    strong = (owner == chosen) | (owner == (partner + parts // 2) % parts)
    return jnp.where(strong, factor * values, values)


def shard_levels(stream_key, shape, pieces, least, high):
    factor_of = 1.0
    for dim, blocks in pieces:
        heights = jax.random.uniform(jax.random.fold_in(jax.random.fold_in(stream_key, 6), dim), (blocks,), jnp.float32, least / len(pieces), high / len(pieces))
        factor_of = factor_of * jnp.repeat(jnp.exp(heights), shape[dim] // blocks).reshape((-1,) + (1,) * (len(shape) - 1 - dim))
    return factor_of


def gaussian(rng, dims, deviation, limit, pieces=(), kind=jnp.bfloat16):
    loudness = shard_levels(rng, dims, pieces, -0.22, 0.18) if pieces else 1.0
    values = jax.random.normal(rng, dims, jnp.float32) * deviation * loudness
    return jnp.minimum(jnp.maximum(values, -limit), limit).astype(kind)


def gaussian_with(own_key, dims, deviation, bound, pieces, heavy, kind=jnp.bfloat16):
    array = deviation * jax.random.normal(own_key, dims, jnp.float32)
    if pieces:
        array = array * shard_levels(own_key, dims, pieces, -0.22, 0.18)
    return jnp.clip(raised(array, jax.random.fold_in(own_key, 3), *heavy), -bound, bound).astype(kind)


def setup_inputs(seed: int = 0) -> dict:
    streams_of = jax.random.split(jax.random.key(seed), 9)
    return {
        "inputs": gaussian(streams_of[0], (BATCH, SEQ, D), 1.0, 6.0, ((0, 128),)),
        "cotangent": gaussian_with(streams_of[1], (BATCH, SEQ, D), 1.0, 24.0, ((0, 128),), (0, 2, 128, 5.5)),
        "lengths": draw_lengths(jax.random.fold_in(streams_of[8], 71), 0),
        "kernel": gaussian(streams_of[3], (KSIZE, D), KSIZE ** -0.5, 1.0, (), jnp.float32),
        "norm_gain": jnp.clip(1.0 + 0.18 * jax.random.normal(streams_of[4], (D,), jnp.float32), 0.1, 1.9),
        "layer_scale": jnp.clip(jnp.exp(jax.random.uniform(streams_of[5], (D,), jnp.float32, math.log(0.3), math.log(1.5))), 0.3, 1.5),
        "w_in": gaussian(streams_of[6], (D, FF), D ** -0.5, 0.21875, ((0, 128), (1, 8))),
        "w_out": gaussian(streams_of[7], (FF, D), FF ** -0.5, 0.109375, ((0, 8), (1, 128))),
    }


def gelu_slope(hidden):
    normal_cdf = 0.5 * (1.0 + jax.scipy.special.erf(hidden * 0.7071067811865476))
    density = jnp.exp(-0.5 * hidden * hidden) * 0.3989422804014327
    return normal_cdf + hidden * density

def reference(inputs, cotangent, lengths, kernel, norm_gain, layer_scale, w_in, w_out):
    seq_len = inputs.shape[1]
    model_width = inputs.shape[2]
    hidden_units = w_in.shape[1]
    groups = N_MP
    local_units = hidden_units // groups
    kernel_taps = kernel.shape[0]
    margin = kernel_taps // 2
    w_in_f = w_in.astype(jnp.float32).reshape(model_width, groups, local_units)
    w_out_f = w_out.astype(jnp.float32).reshape(groups, local_units, model_width)

    def per_spectrum(carry, item):
        acc_in, acc_out, acc_kernel, acc_gain, acc_scale = carry
        spectrum, spec_grad, length = item
        valid_mask = (jnp.arange(seq_len) < length).astype(jnp.float32)[:, None]
        masked = spectrum.astype(jnp.float32) * valid_mask
        padded = jnp.pad(masked, ((margin, margin), (0, 0)))
        conv_out = jnp.zeros_like(masked)
        for offset in range(kernel_taps):
            conv_out = conv_out + kernel[offset] * padded[offset:offset + seq_len]
        centred = conv_out - lax.optimization_barrier(jnp.mean(conv_out, -1, keepdims=True))
        variance = lax.optimization_barrier(jnp.mean(centred * centred, -1, keepdims=True))
        inv_std = lax.rsqrt(variance + 1e-06)
        unit_rows = centred * inv_std
        normed = (unit_rows * norm_gain).astype(jnp.bfloat16)
        hidden = jnp.dot(normed, w_in, preferred_element_type=jnp.float32)
        active = jax.nn.gelu(hidden, approximate=False).astype(jnp.bfloat16)
        partials = jnp.einsum('tgf,gfd->gtd', active.astype(jnp.float32).reshape(seq_len, groups, local_units), w_out_f)
        partials = lax.optimization_barrier(partials.astype(jnp.bfloat16))
        mixed = lax.optimization_barrier(jnp.sum(partials.astype(jnp.float32), 0))
        output = ((masked + layer_scale * mixed) * valid_mask).astype(jnp.bfloat16)
        upstream = spec_grad.astype(jnp.float32) * valid_mask
        scale_term = lax.optimization_barrier(jnp.sum(upstream * mixed, 0))
        scaled_grad = (layer_scale * upstream).astype(jnp.bfloat16)
        out_term = jnp.dot(active.T, scaled_grad, preferred_element_type=jnp.float32)
        act_grad = jnp.dot(scaled_grad, w_out.T, preferred_element_type=jnp.float32)
        hidden_grad = (act_grad * gelu_slope(hidden)).astype(jnp.bfloat16)
        in_term = jnp.dot(normed.T, hidden_grad, preferred_element_type=jnp.float32)
        back_parts = jnp.einsum('tgf,dgf->gtd', hidden_grad.astype(jnp.float32).reshape(seq_len, groups, local_units), w_in_f)
        back_parts = lax.optimization_barrier(back_parts.astype(jnp.bfloat16))
        normed_grad = lax.optimization_barrier(jnp.sum(back_parts.astype(jnp.float32), 0))
        gain_term = lax.optimization_barrier(jnp.sum(normed_grad * unit_rows, 0))
        scaled_norm = normed_grad * norm_gain
        conv_grad = inv_std * (scaled_norm - lax.optimization_barrier(jnp.mean(scaled_norm, -1, keepdims=True)) - unit_rows * lax.optimization_barrier(jnp.mean(scaled_norm * unit_rows, -1, keepdims=True)))
        kernel_term = jnp.stack([lax.optimization_barrier(jnp.sum(conv_grad * padded[offset:offset + seq_len], 0)) for offset in range(kernel_taps)])
        grad_pad = jnp.pad(conv_grad, ((margin, margin), (0, 0)))
        back_conv = jnp.zeros_like(masked)
        for offset in range(kernel_taps):
            first_row = 2 * margin - offset
            back_conv = back_conv + kernel[offset] * grad_pad[first_row:first_row + seq_len]
        input_grad = ((upstream + back_conv) * valid_mask).astype(jnp.bfloat16)
        carry = (acc_in + in_term, acc_out + out_term, acc_kernel + kernel_term, acc_gain + gain_term, acc_scale + scale_term)
        return (carry, (output, input_grad))
    start_carry = (jnp.zeros((model_width, hidden_units), jnp.float32), jnp.zeros((hidden_units, model_width), jnp.float32), jnp.zeros((kernel_taps, model_width), jnp.float32), jnp.zeros((model_width,), jnp.float32), jnp.zeros((model_width,), jnp.float32))
    sums, stacked = lax.scan(per_spectrum, start_carry, (inputs, cotangent, lengths.astype(jnp.int32)))
    return (stacked[0], stacked[1], sums[0], sums[1], sums[2], sums[3], sums[4])
```

```python
import functools

import jax
import jax.numpy as jnp
from jax import lax
from jax.experimental import pallas as pl
from jax.experimental.pallas import tpu as pltpu
from jax.sharding import Mesh, PartitionSpec as P

NX, NY, NC, NZ = 8, 8, 2, 8
PLANE = NX * NY
LANES = 128
TAPS = 31
MARGIN = 15
PAD = 16
BLOCK = 8
BF = jnp.bfloat16
F32 = jnp.float32


def gelu_slope(hidden):
    normal_cdf = 0.5 * (1.0 + jax.scipy.special.erf(hidden * 0.7071067811865476))
    density = jnp.exp(-0.5 * hidden * hidden) * 0.3989422804014327
    return normal_cdf + hidden * density


def whole(shape):
    return pl.BlockSpec(shape, lambda *_: (0,) * len(shape), memory_space=pltpu.VMEM)


def cost(micros):
    moved = int(micros * 3.0e6)
    return pl.CostEstimate(flops=0, transcendentals=0, bytes_accessed=moved)


def smem():
    return pl.BlockSpec(memory_space=pltpu.SMEM)


def shifted_sum(source, taps_of, weights, first, rows):
    total = jnp.zeros((rows, LANES), F32)
    for residue in range(8):
        mine = [(s, tap) for s, tap in taps_of if s % 8 == residue]
        depth = max(s // 8 for s, _ in mine) * 8 + rows
        moved = source(first + residue, depth)
        for s, tap in mine:
            total = total + weights(tap) * moved[s - residue : s - residue + rows]
    return total


def front_kernel(place, lengths, x_ref, cot_ref, taps_ref, gain_ref, scale_ref, normed_ref, scaled_ref, unit_ref, inv_ref, win_ref, pad_ref, conv_ref, std_ref):
    spectra, seq_len, width = x_ref.shape
    span = seq_len // NZ
    z = place[0]
    edge = jnp.zeros((PAD, width), F32)

    def spectrum(b, _):
        length = lengths[b]
        pad_ref[:PAD] = edge
        pad_ref[PAD + seq_len :] = edge

        def fill(i, _):
            at = pl.multiple_of(i * span, span)
            rows = lax.broadcasted_iota(jnp.int32, (span, width), 0) + at
            mask = (rows < length).astype(F32)
            pad_ref[pl.ds(at + PAD, span)] = x_ref[b, pl.ds(at, span)].astype(F32) * mask
            up = cot_ref[b, pl.ds(at, span)].astype(F32) * mask
            scaled_ref[i, b] = (scale_ref[...] * up).astype(BF)
            return 0

        lax.fori_loop(0, NZ, fill, 0)
        win_ref[b] = pad_ref[pl.ds(pl.multiple_of(z * span, span), 2 * span)].astype(BF)

        def columns(j, _):
            lanes = pl.ds(pl.multiple_of(j * LANES, LANES), LANES)
            half = seq_len // 2
            for h in range(2):
                conv_ref[h * half : (h + 1) * half, lanes] = shifted_sum(
                    lambda start, depth: pad_ref[start : start + depth, lanes],
                    [(tap + 1, tap) for tap in range(TAPS)],
                    lambda tap: taps_ref[tap : tap + 1, lanes],
                    h * half,
                    half,
                )
            return 0

        lax.fori_loop(0, width // LANES, columns, 0)

        def norm(i, _):
            at = pl.multiple_of(i * span, span)
            conv = conv_ref[pl.ds(at, span)]
            centred = conv - jnp.mean(conv, -1, keepdims=True)
            inv_std = lax.rsqrt(jnp.mean(centred * centred, -1, keepdims=True) + 1e-06)
            unit = centred * inv_std
            conv_ref[pl.ds(at, span)] = unit
            std_ref[pl.ds(at, span)] = jnp.broadcast_to(inv_std, (span, LANES))
            normed_ref[i, b] = (unit * gain_ref[...]).astype(BF)
            return 0

        lax.fori_loop(0, NZ, norm, 0)
        own = pl.ds(pl.multiple_of(z * span, span), span)
        unit_ref[b] = conv_ref[own]
        inv_ref[b] = std_ref[own]
        return 0

    lax.fori_loop(0, spectra, spectrum, 0)


def front(place, lengths, inputs, cotangent, kernel, gain, scale):
    spectra, seq_len, width = inputs.shape
    span = seq_len // NZ
    blocks = (NZ, spectra, span, width)
    outs = (
        jax.ShapeDtypeStruct(blocks, BF),
        jax.ShapeDtypeStruct(blocks, BF),
        jax.ShapeDtypeStruct((spectra, span, width), F32),
        jax.ShapeDtypeStruct((spectra, span, LANES), F32),
        jax.ShapeDtypeStruct((spectra, 2 * span, width), BF),
    )
    return pl.pallas_call(
        front_kernel,
        in_specs=[smem(), smem()] + [whole(a.shape) for a in (inputs, cotangent, kernel, gain, scale)],
        out_specs=tuple(whole(o.shape) for o in outs),
        out_shape=outs,
        scratch_shapes=[
            pltpu.VMEM((seq_len + 2 * PAD, width), F32),
            pltpu.VMEM((seq_len, width), F32),
            pltpu.VMEM((seq_len, LANES), F32),
        ],
        cost_estimate=cost(16),
        name="front",
    )(place, lengths, inputs, cotangent, kernel, gain, scale)


def norm_back_kernel(parts_ref, unit_ref, inv_ref, win_ref, gain_ref, grad_ref, first_ref, last_ref, sums_ref, win_f):
    spectra, span, width = unit_ref.shape
    gain_sum = jnp.zeros((1, width), F32)
    for b in range(spectra):
        total = parts_ref[0, b].astype(F32)
        for part in range(1, NZ):
            total = total + parts_ref[part, b].astype(F32)
        unit = unit_ref[b]
        gain_sum = gain_sum + jnp.sum(total * unit, 0, keepdims=True)
        g = total * gain_ref[...]
        grad = inv_ref[b][:, :1] * (g - jnp.mean(g, -1, keepdims=True) - unit * jnp.mean(g * unit, -1, keepdims=True))
        grad_ref[b] = grad
        first_ref[b] = grad[:PAD].astype(BF)
        last_ref[b] = grad[span - PAD :].astype(BF)
        win_f[b] = win_ref[b].astype(F32)
    sums_ref[TAPS:, :] = gain_sum

    def columns(j, _):
        lanes = pl.ds(pl.multiple_of(j * LANES, LANES), LANES)
        grads = [grad_ref[b, :, lanes] for b in range(spectra)]
        for residue in range(8):
            moved = [win_f[b, residue : residue + 2 * span - 8, lanes] for b in range(spectra)]
            for s in range(residue, TAPS + 1, 8):
                if s:
                    at = s - residue
                    product = grads[0] * moved[0][at : at + span]
                    for b in range(1, spectra):
                        product = product + grads[b] * moved[b][at : at + span]
                    sums_ref[s - 1 : s, lanes] = jnp.sum(product, 0, keepdims=True)
        return 0

    lax.fori_loop(0, width // LANES, columns, 0)


def norm_back(parts, unit, inv, window, gain):
    spectra, span, width = unit.shape
    outs = (
        jax.ShapeDtypeStruct((spectra, span, width), F32),
        jax.ShapeDtypeStruct((spectra, PAD, width), BF),
        jax.ShapeDtypeStruct((spectra, PAD, width), BF),
        jax.ShapeDtypeStruct((TAPS + 1, width), F32),
    )
    return pl.pallas_call(
        norm_back_kernel,
        in_specs=[whole(a.shape) for a in (parts, unit, inv, window, gain)],
        out_specs=tuple(whole(o.shape) for o in outs),
        out_shape=outs,
        scratch_shapes=[pltpu.VMEM((spectra, 2 * span, width), F32)],
        cost_estimate=cost(3),
        name="norm_back",
    )(parts, unit, inv, window, gain)


def conv_back_kernel(place, lengths, before_ref, grad_ref, after_ref, cot_ref, taps_ref, out_ref, ext_ref):
    spectra, span, width = grad_ref.shape
    start = pl.multiple_of(place[0] * span, span)
    for b in range(spectra):
        ext_ref[b, :PAD] = before_ref[b].astype(F32)
        ext_ref[b, PAD : PAD + span] = grad_ref[b]
        ext_ref[b, PAD + span :] = after_ref[b].astype(F32)

    def columns(j, _):
        lanes = pl.ds(pl.multiple_of(j * LANES, LANES), LANES)
        for b in range(spectra):
            total = shifted_sum(
                lambda first, depth: ext_ref[b, first : first + depth, lanes],
                [(TAPS - tap, tap) for tap in range(TAPS)],
                lambda tap: taps_ref[tap : tap + 1, lanes],
                0,
                span,
            )
            rows = lax.broadcasted_iota(jnp.int32, (span, LANES), 0) + start
            mask = (rows < lengths[b]).astype(F32)
            up = cot_ref[b, pl.ds(start, span), lanes].astype(F32) * mask
            out_ref[b, :, lanes] = ((up + total) * mask).astype(BF)
        return 0

    lax.fori_loop(0, width // LANES, columns, 0)


def conv_back(place, lengths, before, grad, after, cotangent, kernel):
    spectra, span, width = grad.shape
    out = jax.ShapeDtypeStruct((spectra, span, width), BF)
    return pl.pallas_call(
        conv_back_kernel,
        in_specs=[smem(), smem()] + [whole(a.shape) for a in (before, grad, after, cotangent, kernel)],
        out_specs=whole(out.shape),
        out_shape=out,
        scratch_shapes=[pltpu.VMEM((spectra, span + 2 * PAD, width), F32)],
        cost_estimate=cost(3),
        name="conv_back",
    )(place, lengths, before, grad, after, cotangent, kernel)


def close_kernel(place, lengths, parts_ref, x_ref, scale_ref, out_ref):
    spectra, span, width = out_ref.shape
    start = pl.multiple_of(place[0] * span, span)
    for b in range(spectra):
        total = parts_ref[0, b].astype(F32)
        for part in range(1, NZ):
            total = total + parts_ref[part, b].astype(F32)
        rows = lax.broadcasted_iota(jnp.int32, (span, width), 0) + start
        mask = (rows < lengths[b]).astype(F32)
        own = x_ref[b, pl.ds(start, span)].astype(F32) * mask
        out_ref[b] = ((own + scale_ref[...] * total) * mask).astype(BF)


def close(place, lengths, parts, inputs, scale):
    _, spectra, span, width = parts.shape
    out = jax.ShapeDtypeStruct((spectra, span, width), BF)
    return pl.pallas_call(
        close_kernel,
        in_specs=[smem(), smem()] + [whole(a.shape) for a in (parts, inputs, scale)],
        out_specs=whole(out.shape),
        out_shape=out,
        cost_estimate=cost(2),
        name="close",
    )(place, lengths, parts, inputs, scale)


def place_kernel(place, *refs):
    blocks, out_ref = refs[:-1], refs[-1]
    spectra, span, _ = blocks[0].shape
    for step, block in enumerate(blocks):
        at = pl.multiple_of(((place[0] + step) % NZ) * span, span)
        for b in range(spectra):
            out_ref[b, pl.ds(at, span)] = block[b]


def gather_rows(place, own):
    spectra, span, width = own.shape
    blocks = [own]
    for step in range(1, NZ):
        blocks.append(lax.ppermute(own, "mp", [(i, (i - step) % NZ) for i in range(NZ)]))
    out = jax.ShapeDtypeStruct((spectra, span * NZ, width), own.dtype)
    return pl.pallas_call(
        place_kernel,
        in_specs=[smem()] + [whole(own.shape)] * NZ,
        out_specs=whole(out.shape),
        out_shape=out,
        cost_estimate=cost(1),
        name="place",
    )(place, *blocks)


def swap_cores(value):
    return lax.ppermute(value, "c", [(0, 1), (1, 0)])


def order_matrix(width, share):
    slot = jnp.arange(NC * PLANE * BLOCK, dtype=jnp.int32)
    row = slot % BLOCK
    plane = (slot // BLOCK) % PLANE
    core = (slot // (BLOCK * PLANE) + lax.axis_index("c")) % NC
    natural = jnp.where(row < share, (plane * NC + core) * share + row, -1)
    return (jnp.arange(width, dtype=jnp.int32)[:, None] == natural[None, :]).astype(BF)


def core_sum(terms):
    half = PLANE * BLOCK
    return (terms[:half].astype(F32) + swap_cores(terms[half:]).astype(F32)).astype(BF)


def body(inputs, cotangent, lengths, kernel, norm_gain, layer_scale, w_in, w_out):
    spectra, seq_len, width = inputs.shape
    units = w_in.shape[1]
    share = w_in.shape[0]
    tokens = spectra * seq_len
    span = seq_len // NZ
    place = lax.axis_index("mp").astype(jnp.int32).reshape(1)
    gain = norm_gain[None, :]
    scale = layer_scale[None, :]

    both = jnp.pad(jnp.concatenate((w_in, w_out.T), 1), ((0, BLOCK - share), (0, 0)))
    both = lax.all_to_all(jnp.broadcast_to(both[None], (PLANE, BLOCK, 2 * units)), ("x", "y"), 0, 0)
    normed, scaled, unit_own, inv_own, window = front(place, lengths, inputs, cotangent, kernel, gain, scale)
    both, normed = lax.optimization_barrier((both, normed))
    both = both.reshape(PLANE * BLOCK, 2 * units)
    arranged = jnp.concatenate((both, swap_cores(both)), 0)
    order = order_matrix(width, share)
    normed = normed.reshape(tokens, width)
    scaled = scaled.reshape(tokens, width)

    full = jnp.dot(order, arranged, preferred_element_type=F32).astype(BF)
    full_in, full_out = full[:, :units], full[:, units:]
    hidden = jnp.dot(normed, full_in, preferred_element_type=F32)
    act_grad = jnp.dot(scaled, full_out, preferred_element_type=F32)
    hidden_grad = (act_grad * gelu_slope(hidden)).astype(BF)
    active = jax.nn.gelu(hidden, approximate=False).astype(BF)
    flip = (((1,), (1,)), ((), ()))
    firsts = (((0,), (0,)), ((), ()))
    blocks = (NZ, spectra, span, width)
    back_part = lax.dot_general(hidden_grad, full_in, flip, preferred_element_type=F32).astype(BF)
    back_parts = lax.all_to_all(back_part.reshape(blocks), "mp", 0, 0)

    mixed_part = lax.dot_general(active, full_out, flip, preferred_element_type=F32).astype(BF)
    in_term = lax.dot_general(normed, hidden_grad, firsts, preferred_element_type=F32).astype(BF)
    out_term = lax.dot_general(scaled, active, firsts, preferred_element_type=F32).astype(BF)
    terms = jnp.concatenate((in_term, out_term), 1)
    terms = lax.dot_general(order, terms, firsts, preferred_element_type=F32).astype(BF)
    terms = core_sum(terms)
    mixed_blocks = jnp.swapaxes(mixed_part.reshape(blocks), 0, 1).reshape(spectra, seq_len, width)
    positions = jnp.arange(seq_len, dtype=jnp.int32)
    valid_mask = (positions[None, :] < lengths[:, None]).astype(F32)[:, :, None]
    scale_part = jnp.sum(cotangent.astype(F32) * valid_mask * mixed_blocks.astype(F32), (0, 1))

    conv_grad, first, last, sums = norm_back(back_parts, unit_own, inv_own, window, gain)
    before = lax.ppermute(last, "mp", [(i, i + 1) for i in range(NZ - 1)])
    after = lax.ppermute(first, "mp", [(i + 1, i) for i in range(NZ - 1)])
    small = jnp.concatenate((sums, scale_part[None, :]), 0).astype(BF)
    small = lax.dot_general(order, small, (((0,), (1,)), ((), ())), preferred_element_type=F32).astype(BF)
    small = core_sum(jnp.pad(small, ((0, 0), (0, LANES - TAPS - 2))))

    terms = jnp.concatenate((terms, small), 1).reshape(PLANE, BLOCK, -1)
    terms = lax.all_to_all(terms, ("x", "y"), 0, 0)

    own_grad = conv_back(place, lengths, before, conv_grad, after, cotangent, kernel)
    input_grad = gather_rows(place, own_grad)

    terms, mixed_part, input_grad = lax.optimization_barrier((terms, mixed_part, input_grad))
    mixed_parts = lax.all_to_all(mixed_part.reshape(blocks), "mp", 0, 0)
    terms = jnp.sum(terms.astype(F32), 0)[:share]
    grads = terms[:, : 2 * units]
    small = lax.psum(terms[:, 2 * units : 2 * units + TAPS + 2], "mp").T
    output = close(place, lengths, mixed_parts, inputs, scale)
    return (
        output,
        input_grad,
        grads[:, :units],
        grads[:, units:].T,
        small[:TAPS],
        small[TAPS],
        small[TAPS + 1],
    )


def solution(mesh):
    fine = Mesh(mesh.devices.reshape(NX, NY, NC, NZ), ("x", "y", "c", "mp"))
    dp = ("x", "y", "c")
    placed = (
        P(dp, None, None),
        P(dp, None, None),
        P(dp),
        P(),
        P(),
        P(),
        P(dp, "mp"),
        P("mp", dp),
    )
    return jax.shard_map(
        body,
        mesh=fine,
        in_specs=placed,
        out_specs=(
            P(dp, "mp", None),
            P(dp, None, None),
            P(dp, "mp"),
            P("mp", dp),
            P(None, dp),
            P(dp),
            P(dp),
        ),
        check_vma=False,
    )
```

```python
import functools

import jax
import jax.numpy as jnp
from jax import lax
from jax.experimental import pallas as pl
from jax.experimental.pallas import tpu as pltpu
from jax.sharding import Mesh, PartitionSpec as P

NX, NY, NC, NZ = 8, 8, 2, 8
PLANE = NX * NY
LANES = 128
TAPS = 31
MARGIN = 15
PAD = 16
BLOCK = 8
BF = jnp.bfloat16
F32 = jnp.float32


def gelu_slope(hidden):
    normal_cdf = 0.5 * (1.0 + jax.scipy.special.erf(hidden * 0.7071067811865476))
    density = jnp.exp(-0.5 * hidden * hidden) * 0.3989422804014327
    return normal_cdf + hidden * density


def whole(shape):
    return pl.BlockSpec(shape, lambda *_: (0,) * len(shape), memory_space=pltpu.VMEM)


def cost(micros):
    moved = int(micros * 3.0e6)
    return pl.CostEstimate(flops=0, transcendentals=0, bytes_accessed=moved)


def smem():
    return pl.BlockSpec(memory_space=pltpu.SMEM)


def shifted_sum(source, taps_of, weights, first, rows):
    total = jnp.zeros((rows, LANES), F32)
    for residue in range(8):
        mine = [(s, tap) for s, tap in taps_of if s % 8 == residue]
        depth = max(s // 8 for s, _ in mine) * 8 + rows
        moved = source(first + residue, depth)
        for s, tap in mine:
            total = total + weights(tap) * moved[s - residue : s - residue + rows]
    return total


def front_kernel(place, lengths, x_ref, cot_ref, taps_ref, gain_ref, scale_ref, normed_ref, scaled_ref, unit_ref, inv_ref, win_ref, pad_ref, conv_ref, std_ref):
    spectra, seq_len, width = x_ref.shape
    span = seq_len // NZ
    z = place[0]
    edge = jnp.zeros((PAD, width), F32)

    def spectrum(b, _):
        length = lengths[b]
        pad_ref[:PAD] = edge
        pad_ref[PAD + seq_len :] = edge

        def fill(i, _):
            at = pl.multiple_of(i * span, span)
            rows = lax.broadcasted_iota(jnp.int32, (span, width), 0) + at
            mask = (rows < length).astype(F32)
            pad_ref[pl.ds(at + PAD, span)] = x_ref[b, pl.ds(at, span)].astype(F32) * mask
            up = cot_ref[b, pl.ds(at, span)].astype(F32) * mask
            scaled_ref[i, b] = (scale_ref[...] * up).astype(BF)
            return 0

        lax.fori_loop(0, NZ, fill, 0)
        win_ref[b] = pad_ref[pl.ds(pl.multiple_of(z * span, span), 2 * span)].astype(BF)

        def columns(j, _):
            lanes = pl.ds(pl.multiple_of(j * LANES, LANES), LANES)
            half = seq_len // 2
            for h in range(2):
                conv_ref[h * half : (h + 1) * half, lanes] = shifted_sum(
                    lambda start, depth: pad_ref[start : start + depth, lanes],
                    [(tap + 1, tap) for tap in range(TAPS)],
                    lambda tap: taps_ref[tap : tap + 1, lanes],
                    h * half,
                    half,
                )
            return 0

        lax.fori_loop(0, width // LANES, columns, 0)

        def norm(i, _):
            at = pl.multiple_of(i * span, span)
            conv = conv_ref[pl.ds(at, span)]
            centred = conv - jnp.mean(conv, -1, keepdims=True)
            inv_std = lax.rsqrt(jnp.mean(centred * centred, -1, keepdims=True) + 1e-06)
            unit = centred * inv_std
            conv_ref[pl.ds(at, span)] = unit
            std_ref[pl.ds(at, span)] = jnp.broadcast_to(inv_std, (span, LANES))
            normed_ref[i, b] = (unit * gain_ref[...]).astype(BF)
            return 0

        lax.fori_loop(0, NZ, norm, 0)
        own = pl.ds(pl.multiple_of(z * span, span), span)
        unit_ref[b] = conv_ref[own]
        inv_ref[b] = std_ref[own]
        return 0

    lax.fori_loop(0, spectra, spectrum, 0)


def front(place, lengths, inputs, cotangent, kernel, gain, scale):
    spectra, seq_len, width = inputs.shape
    span = seq_len // NZ
    blocks = (NZ, spectra, span, width)
    outs = (
        jax.ShapeDtypeStruct(blocks, BF),
        jax.ShapeDtypeStruct(blocks, BF),
        jax.ShapeDtypeStruct((spectra, span, width), F32),
        jax.ShapeDtypeStruct((spectra, span, LANES), F32),
        jax.ShapeDtypeStruct((spectra, 2 * span, width), BF),
    )
    return pl.pallas_call(
        front_kernel,
        in_specs=[smem(), smem()] + [whole(a.shape) for a in (inputs, cotangent, kernel, gain, scale)],
        out_specs=tuple(whole(o.shape) for o in outs),
        out_shape=outs,
        scratch_shapes=[
            pltpu.VMEM((seq_len + 2 * PAD, width), F32),
            pltpu.VMEM((seq_len, width), F32),
            pltpu.VMEM((seq_len, LANES), F32),
        ],
        cost_estimate=cost(16),
        name="front",
    )(place, lengths, inputs, cotangent, kernel, gain, scale)


def norm_back_kernel(parts_ref, unit_ref, inv_ref, win_ref, gain_ref, grad_ref, first_ref, last_ref, sums_ref, win_f):
    spectra, span, width = unit_ref.shape
    gain_sum = jnp.zeros((1, width), F32)
    for b in range(spectra):
        total = parts_ref[0, b].astype(F32)
        for part in range(1, NZ):
            total = total + parts_ref[part, b].astype(F32)
        unit = unit_ref[b]
        gain_sum = gain_sum + jnp.sum(total * unit, 0, keepdims=True)
        g = total * gain_ref[...]
        grad = inv_ref[b][:, :1] * (g - jnp.mean(g, -1, keepdims=True) - unit * jnp.mean(g * unit, -1, keepdims=True))
        grad_ref[b] = grad
        first_ref[b] = grad[:PAD].astype(BF)
        last_ref[b] = grad[span - PAD :].astype(BF)
        win_f[b] = win_ref[b].astype(F32)
    sums_ref[TAPS:, :] = gain_sum

    def columns(j, _):
        lanes = pl.ds(pl.multiple_of(j * LANES, LANES), LANES)
        grads = [grad_ref[b, :, lanes] for b in range(spectra)]
        for residue in range(8):
            moved = [win_f[b, residue : residue + 2 * span - 8, lanes] for b in range(spectra)]
            for s in range(residue, TAPS + 1, 8):
                if s:
                    at = s - residue
                    product = grads[0] * moved[0][at : at + span]
                    for b in range(1, spectra):
                        product = product + grads[b] * moved[b][at : at + span]
                    sums_ref[s - 1 : s, lanes] = jnp.sum(product, 0, keepdims=True)
        return 0

    lax.fori_loop(0, width // LANES, columns, 0)


def norm_back(parts, unit, inv, window, gain):
    spectra, span, width = unit.shape
    outs = (
        jax.ShapeDtypeStruct((spectra, span, width), F32),
        jax.ShapeDtypeStruct((spectra, PAD, width), BF),
        jax.ShapeDtypeStruct((spectra, PAD, width), BF),
        jax.ShapeDtypeStruct((TAPS + 1, width), F32),
    )
    return pl.pallas_call(
        norm_back_kernel,
        in_specs=[whole(a.shape) for a in (parts, unit, inv, window, gain)],
        out_specs=tuple(whole(o.shape) for o in outs),
        out_shape=outs,
        scratch_shapes=[pltpu.VMEM((spectra, 2 * span, width), F32)],
        cost_estimate=cost(3),
        name="norm_back",
    )(parts, unit, inv, window, gain)


def conv_back_kernel(place, lengths, before_ref, grad_ref, after_ref, cot_ref, taps_ref, out_ref, ext_ref):
    spectra, span, width = grad_ref.shape
    start = pl.multiple_of(place[0] * span, span)
    for b in range(spectra):
        ext_ref[b, :PAD] = before_ref[b].astype(F32)
        ext_ref[b, PAD : PAD + span] = grad_ref[b]
        ext_ref[b, PAD + span :] = after_ref[b].astype(F32)

    def columns(j, _):
        lanes = pl.ds(pl.multiple_of(j * LANES, LANES), LANES)
        for b in range(spectra):
            total = shifted_sum(
                lambda first, depth: ext_ref[b, first : first + depth, lanes],
                [(TAPS - tap, tap) for tap in range(TAPS)],
                lambda tap: taps_ref[tap : tap + 1, lanes],
                0,
                span,
            )
            rows = lax.broadcasted_iota(jnp.int32, (span, LANES), 0) + start
            mask = (rows < lengths[b]).astype(F32)
            up = cot_ref[b, pl.ds(start, span), lanes].astype(F32) * mask
            out_ref[b, :, lanes] = ((up + total) * mask).astype(BF)
        return 0

    lax.fori_loop(0, width // LANES, columns, 0)


def conv_back(place, lengths, before, grad, after, cotangent, kernel):
    spectra, span, width = grad.shape
    out = jax.ShapeDtypeStruct((spectra, span, width), BF)
    return pl.pallas_call(
        conv_back_kernel,
        in_specs=[smem(), smem()] + [whole(a.shape) for a in (before, grad, after, cotangent, kernel)],
        out_specs=whole(out.shape),
        out_shape=out,
        scratch_shapes=[pltpu.VMEM((spectra, span + 2 * PAD, width), F32)],
        cost_estimate=cost(3),
        name="conv_back",
    )(place, lengths, before, grad, after, cotangent, kernel)


def close_kernel(place, lengths, parts_ref, x_ref, scale_ref, out_ref):
    spectra, span, width = out_ref.shape
    start = pl.multiple_of(place[0] * span, span)
    for b in range(spectra):
        total = parts_ref[0, b].astype(F32)
        for part in range(1, NZ):
            total = total + parts_ref[part, b].astype(F32)
        rows = lax.broadcasted_iota(jnp.int32, (span, width), 0) + start
        mask = (rows < lengths[b]).astype(F32)
        own = x_ref[b, pl.ds(start, span)].astype(F32) * mask
        out_ref[b] = ((own + scale_ref[...] * total) * mask).astype(BF)


def close(place, lengths, parts, inputs, scale):
    _, spectra, span, width = parts.shape
    out = jax.ShapeDtypeStruct((spectra, span, width), BF)
    return pl.pallas_call(
        close_kernel,
        in_specs=[smem(), smem()] + [whole(a.shape) for a in (parts, inputs, scale)],
        out_specs=whole(out.shape),
        out_shape=out,
        cost_estimate=cost(2),
        name="close",
    )(place, lengths, parts, inputs, scale)


def swap_cores(value):
    return lax.ppermute(value, "c", [(0, 1), (1, 0)])


def order_matrix(width, share):
    slot = jnp.arange(NC * PLANE * BLOCK, dtype=jnp.int32)
    row = slot % BLOCK
    plane = (slot // BLOCK) % PLANE
    core = (slot // (BLOCK * PLANE) + lax.axis_index("c")) % NC
    natural = jnp.where(row < share, (plane * NC + core) * share + row, -1)
    return (jnp.arange(width, dtype=jnp.int32)[:, None] == natural[None, :]).astype(BF)


def core_sum(terms):
    half = PLANE * BLOCK
    return (terms[:half].astype(F32) + swap_cores(terms[half:]).astype(F32)).astype(BF)


def body(inputs, cotangent, lengths, kernel, norm_gain, layer_scale, w_in, w_out):
    spectra, seq_len, width = inputs.shape
    units = w_in.shape[1]
    share = w_in.shape[0]
    tokens = spectra * seq_len
    span = seq_len // NZ
    place = lax.axis_index("mp").astype(jnp.int32).reshape(1)
    gain = norm_gain[None, :]
    scale = layer_scale[None, :]

    both = jnp.pad(jnp.concatenate((w_in, w_out.T), 1), ((0, BLOCK - share), (0, 0)))
    both = lax.all_to_all(jnp.broadcast_to(both[None], (PLANE, BLOCK, 2 * units)), ("x", "y"), 0, 0)
    normed, scaled, unit_own, inv_own, window = front(place, lengths, inputs, cotangent, kernel, gain, scale)
    both, normed = lax.optimization_barrier((both, normed))
    both = both.reshape(PLANE * BLOCK, 2 * units)
    arranged = jnp.concatenate((both, swap_cores(both)), 0)
    order = order_matrix(width, share)
    normed = normed.reshape(tokens, width)
    scaled = scaled.reshape(tokens, width)

    full = jnp.dot(order, arranged, preferred_element_type=F32).astype(BF)
    full_in, full_out = full[:, :units], full[:, units:]
    hidden = jnp.dot(normed, full_in, preferred_element_type=F32)
    act_grad = jnp.dot(scaled, full_out, preferred_element_type=F32)
    hidden_grad = (act_grad * gelu_slope(hidden)).astype(BF)
    active = jax.nn.gelu(hidden, approximate=False).astype(BF)
    flip = (((1,), (1,)), ((), ()))
    firsts = (((0,), (0,)), ((), ()))
    blocks = (NZ, spectra, span, width)
    back_part = lax.dot_general(hidden_grad, full_in, flip, preferred_element_type=F32).astype(BF)
    back_parts = lax.all_to_all(back_part.reshape(blocks), "mp", 0, 0)

    mixed_part = lax.dot_general(active, full_out, flip, preferred_element_type=F32).astype(BF)
    in_term = lax.dot_general(normed, hidden_grad, firsts, preferred_element_type=F32).astype(BF)
    out_term = lax.dot_general(scaled, active, firsts, preferred_element_type=F32).astype(BF)
    terms = jnp.concatenate((in_term, out_term), 1)
    terms = lax.dot_general(order, terms, firsts, preferred_element_type=F32).astype(BF)
    terms = core_sum(terms)
    mixed_blocks = jnp.swapaxes(mixed_part.reshape(blocks), 0, 1).reshape(spectra, seq_len, width)
    positions = jnp.arange(seq_len, dtype=jnp.int32)
    valid_mask = (positions[None, :] < lengths[:, None]).astype(F32)[:, :, None]
    scale_part = jnp.sum(cotangent.astype(F32) * valid_mask * mixed_blocks.astype(F32), (0, 1))

    back_parts, mixed_part = lax.optimization_barrier((back_parts, mixed_part))
    mixed_parts = lax.all_to_all(mixed_part.reshape(blocks), "mp", 0, 0)

    conv_grad, first, last, sums = norm_back(back_parts, unit_own, inv_own, window, gain)
    before = lax.ppermute(last, "mp", [(i, i + 1) for i in range(NZ - 1)])
    after = lax.ppermute(first, "mp", [(i + 1, i) for i in range(NZ - 1)])
    small = jnp.concatenate((sums, scale_part[None, :]), 0).astype(BF)
    small = lax.dot_general(order, small, (((0,), (1,)), ((), ())), preferred_element_type=F32).astype(BF)
    small = core_sum(jnp.pad(small, ((0, 0), (0, LANES - TAPS - 2))))

    own_grad = conv_back(place, lengths, before, conv_grad, after, cotangent, kernel)

    terms = jnp.concatenate((terms, small), 1).reshape(PLANE, BLOCK, -1)
    terms, own_grad, mixed_parts = lax.optimization_barrier((terms, own_grad, mixed_parts))
    terms = lax.all_to_all(terms, ("x", "y"), 0, 0)
    rows = lax.all_gather(own_grad, "mp", axis=0, tiled=False)
    terms, rows, mixed_parts = lax.optimization_barrier((terms, rows, mixed_parts))
    input_grad = jnp.swapaxes(rows, 0, 1).reshape(spectra, seq_len, width)
    output = close(place, lengths, mixed_parts, inputs, scale)
    terms = jnp.sum(terms.astype(F32), 0)
    grads = terms[:share, : 2 * units]
    small = jnp.broadcast_to(terms[None, :, 2 * units :], (NZ, BLOCK, LANES))
    small = jnp.sum(lax.all_to_all(small, "mp", 0, 0), 0)[:share, : TAPS + 2].T
    return (
        output,
        input_grad,
        grads[:, :units],
        grads[:, units:].T,
        small[:TAPS],
        small[TAPS],
        small[TAPS + 1],
    )


def solution(mesh):
    fine = Mesh(mesh.devices.reshape(NX, NY, NC, NZ), ("x", "y", "c", "mp"))
    dp = ("x", "y", "c")
    placed = (
        P(dp, None, None),
        P(dp, None, None),
        P(dp),
        P(),
        P(),
        P(),
        P(dp, "mp"),
        P("mp", dp),
    )
    return jax.shard_map(
        body,
        mesh=fine,
        in_specs=placed,
        out_specs=(
            P(dp, "mp", None),
            P(dp, None, None),
            P(dp, "mp"),
            P("mp", dp),
            P(None, dp),
            P(dp),
            P(dp),
        ),
        check_vma=False,
    )
```

```python
import jax
import jax.numpy as jnp
from jax import lax
from jax.experimental import pallas as pl
from jax.experimental.pallas import tpu as pltpu
from jax.sharding import Mesh, PartitionSpec as P


NX, NY, NC, NZ = 8, 8, 2, 8
PLANE = NX * NY
LANES = 128
TAPS = 31
PAD = 16
BLOCK = 8
BF = jnp.bfloat16
F32 = jnp.float32


def gelu_slope(hidden):
    normal_cdf = 0.5 * (1.0 + jax.scipy.special.erf(hidden * 0.7071067811865476))
    density = jnp.exp(-0.5 * hidden * hidden) * 0.3989422804014327
    return normal_cdf + hidden * density


def whole(shape):
    return pl.BlockSpec(shape, lambda *_: (0,) * len(shape), memory_space=pltpu.VMEM)


def cost(micros):
    moved = int(micros * 3.0e6)
    return pl.CostEstimate(flops=0, transcendentals=0, bytes_accessed=moved)


def smem():
    return pl.BlockSpec(memory_space=pltpu.SMEM)


def shifted_sum(source, taps_of, weights, first, rows):
    total = jnp.zeros((rows, LANES), F32)
    for residue in range(8):
        mine = [(s, tap) for s, tap in taps_of if s % 8 == residue]
        depth = max(s // 8 for s, _ in mine) * 8 + rows
        moved = source(first + residue, depth)
        for s, tap in mine:
            total = total + weights(tap) * moved[s - residue : s - residue + rows]
    return total


def front_kernel(place, lengths, x_ref, cot_ref, taps_ref, rows_ref, normed_ref, scaled_ref, up_ref, unit_ref, inv_ref, win_ref, pad_ref, conv_ref, std_ref):
    spectra, seq_len, width = x_ref.shape
    span = seq_len // NZ
    z = place[0]
    edge = jnp.zeros((PAD, width), F32)

    def spectrum(b, _):
        length = lengths[b]
        pad_ref[:PAD] = edge
        pad_ref[PAD + seq_len :] = edge

        def fill(i, _):
            at = pl.multiple_of(i * span, span)
            rows = lax.broadcasted_iota(jnp.int32, (span, width), 0) + at
            mask = (rows < length).astype(F32)
            pad_ref[pl.ds(at + PAD, span)] = x_ref[b, pl.ds(at, span)].astype(F32) * mask
            up = cot_ref[b, pl.ds(at, span)].astype(F32) * mask
            scaled_ref[i, b] = (rows_ref[1:2] * up).astype(BF)
            up_ref[i, b] = up.astype(BF)
            return 0

        lax.fori_loop(0, NZ, fill, 0)
        win_ref[b] = pad_ref[pl.ds(pl.multiple_of(z * span, span), 2 * span)].astype(BF)

        def columns(j, _):
            lanes = pl.ds(pl.multiple_of(j * LANES, LANES), LANES)
            half = seq_len // 2
            for h in range(2):
                conv_ref[h * half : (h + 1) * half, lanes] = shifted_sum(
                    lambda start, depth: pad_ref[start : start + depth, lanes],
                    [(tap + 1, tap) for tap in range(TAPS)],
                    lambda tap: taps_ref[tap : tap + 1, lanes],
                    h * half,
                    half,
                )
            return 0

        lax.fori_loop(0, width // LANES, columns, 0)

        def norm(i, _):
            at = pl.multiple_of(i * span, span)
            conv = conv_ref[pl.ds(at, span)]
            centred = conv - jnp.mean(conv, -1, keepdims=True)
            inv_std = lax.rsqrt(jnp.mean(centred * centred, -1, keepdims=True) + 1e-06)
            unit = centred * inv_std
            conv_ref[pl.ds(at, span)] = unit
            std_ref[pl.ds(at, span)] = jnp.broadcast_to(inv_std, (span, LANES))
            normed_ref[i, b] = (unit * rows_ref[:1]).astype(BF)
            return 0

        lax.fori_loop(0, NZ, norm, 0)
        own = pl.ds(pl.multiple_of(z * span, span), span)
        unit_ref[b] = conv_ref[own]
        inv_ref[b] = std_ref[own]
        return 0

    lax.fori_loop(0, spectra, spectrum, 0)


def front(place, lengths, inputs, cotangent, kernel, rows):
    spectra, seq_len, width = inputs.shape
    span = seq_len // NZ
    blocks = (NZ, spectra, span, width)
    outs = (
        jax.ShapeDtypeStruct(blocks, BF),
        jax.ShapeDtypeStruct(blocks, BF),
        jax.ShapeDtypeStruct(blocks, BF),
        jax.ShapeDtypeStruct((spectra, span, width), F32),
        jax.ShapeDtypeStruct((spectra, span, LANES), F32),
        jax.ShapeDtypeStruct((spectra, 2 * span, width), BF),
    )
    return pl.pallas_call(
        front_kernel,
        in_specs=[smem(), smem()] + [whole(a.shape) for a in (inputs, cotangent, kernel, rows)],
        out_specs=tuple(whole(o.shape) for o in outs),
        out_shape=outs,
        scratch_shapes=[
            pltpu.VMEM((seq_len + 2 * PAD, width), F32),
            pltpu.VMEM((seq_len, width), F32),
            pltpu.VMEM((seq_len, LANES), F32),
        ],
        cost_estimate=cost(16),
        name="front",
    )(place, lengths, inputs, cotangent, kernel, rows)


def norm_back_kernel(parts_ref, unit_ref, inv_ref, rows_ref, grad_ref, first_ref, last_ref, gain_ref):
    spectra, span, width = unit_ref.shape
    gain_sum = jnp.zeros((1, width), F32)
    for b in range(spectra):
        total = parts_ref[0, b].astype(F32)
        for part in range(1, NZ):
            total = total + parts_ref[part, b].astype(F32)
        unit = unit_ref[b]
        gain_sum = gain_sum + jnp.sum(total * unit, 0, keepdims=True)
        g = total * rows_ref[:1]
        grad = inv_ref[b][:, :1] * (g - jnp.mean(g, -1, keepdims=True) - unit * jnp.mean(g * unit, -1, keepdims=True))
        grad_ref[b] = grad
        first_ref[b] = grad[:PAD].astype(BF)
        last_ref[b] = grad[span - PAD :].astype(BF)
    gain_ref[...] = gain_sum


def norm_back(parts, unit, inv, rows):
    spectra, span, width = unit.shape
    outs = (
        jax.ShapeDtypeStruct((spectra, span, width), F32),
        jax.ShapeDtypeStruct((spectra, PAD, width), BF),
        jax.ShapeDtypeStruct((spectra, PAD, width), BF),
        jax.ShapeDtypeStruct((1, width), F32),
    )
    return pl.pallas_call(
        norm_back_kernel,
        in_specs=[whole(a.shape) for a in (parts, unit, inv, rows)],
        out_specs=tuple(whole(o.shape) for o in outs),
        out_shape=outs,
        cost_estimate=cost(2),
        name="norm_back",
    )(parts, unit, inv, rows)


def pack_kernel(grad_ref, win_ref, gain_ref, scale_ref, order_ref, terms_ref, out_ref, win_f, sums_ref):
    spectra, span, width = grad_ref.shape
    half = terms_ref.shape[0]
    for b in range(spectra):
        win_f[b] = win_ref[b].astype(F32)
    sums_ref[...] = jnp.zeros(sums_ref.shape, F32)
    sums_ref[TAPS : TAPS + 1] = gain_ref[...]
    sums_ref[TAPS + 1 : TAPS + 2] = scale_ref[...]

    def columns(j, _):
        lanes = pl.ds(pl.multiple_of(j * LANES, LANES), LANES)
        grads = [grad_ref[b, :, lanes] for b in range(spectra)]
        for residue in range(8):
            moved = [win_f[b, residue : residue + 2 * span - 8, lanes] for b in range(spectra)]
            for s in range(residue, TAPS + 1, 8):
                if s:
                    at = s - residue
                    product = grads[0] * moved[0][at : at + span]
                    for b in range(1, spectra):
                        product = product + grads[b] * moved[b][at : at + span]
                    sums_ref[s - 1 : s, lanes] = jnp.sum(product, 0, keepdims=True)
        return 0

    lax.fori_loop(0, width // LANES, columns, 0)
    out_ref[:, :width] = terms_ref[...]
    sums = sums_ref[...].astype(BF)
    for core in range(NC):
        turned = lax.dot_general(
            order_ref[core * half : (core + 1) * half], sums, (((1,), (1,)), ((), ())), preferred_element_type=F32
        )
        out_ref[:, width + core * LANES : width + (core + 1) * LANES] = turned.astype(BF)


def pack(grad, window, gain_sum, scale_sum, order, terms):
    spectra, span, width = grad.shape
    out = jax.ShapeDtypeStruct((terms.shape[0], width + NC * LANES), BF)
    return pl.pallas_call(
        pack_kernel,
        in_specs=[whole(a.shape) for a in (grad, window, gain_sum, scale_sum, order, terms)],
        out_specs=whole(out.shape),
        out_shape=out,
        scratch_shapes=[pltpu.VMEM((spectra, 2 * span, width), F32), pltpu.VMEM((LANES, width), F32)],
        cost_estimate=cost(3),
        name="pack",
    )(grad, window, gain_sum, scale_sum, order, terms)


def conv_back_kernel(place, lengths, before_ref, grad_ref, after_ref, cot_ref, taps_ref, out_ref, ext_ref):
    spectra, span, width = grad_ref.shape
    start = pl.multiple_of(place[0] * span, span)
    for b in range(spectra):
        ext_ref[b, :PAD] = before_ref[b].astype(F32)
        ext_ref[b, PAD : PAD + span] = grad_ref[b]
        ext_ref[b, PAD + span :] = after_ref[b].astype(F32)

    def columns(j, _):
        lanes = pl.ds(pl.multiple_of(j * LANES, LANES), LANES)
        for b in range(spectra):
            total = shifted_sum(
                lambda first, depth: ext_ref[b, first : first + depth, lanes],
                [(TAPS - tap, tap) for tap in range(TAPS)],
                lambda tap: taps_ref[tap : tap + 1, lanes],
                0,
                span,
            )
            rows = lax.broadcasted_iota(jnp.int32, (span, LANES), 0) + start
            mask = (rows < lengths[b]).astype(F32)
            up = cot_ref[b, pl.ds(start, span), lanes].astype(F32) * mask
            out_ref[b, :, lanes] = ((up + total) * mask).astype(BF)
        return 0

    lax.fori_loop(0, width // LANES, columns, 0)


def conv_back(place, lengths, before, grad, after, cotangent, kernel):
    spectra, span, width = grad.shape
    out = jax.ShapeDtypeStruct((spectra, span, width), BF)
    return pl.pallas_call(
        conv_back_kernel,
        in_specs=[smem(), smem()] + [whole(a.shape) for a in (before, grad, after, cotangent, kernel)],
        out_specs=whole(out.shape),
        out_shape=out,
        scratch_shapes=[pltpu.VMEM((spectra, span + 2 * PAD, width), F32)],
        cost_estimate=cost(3),
        name="conv_back",
    )(place, lengths, before, grad, after, cotangent, kernel)


def close_kernel(place, lengths, parts_ref, x_ref, rows_ref, out_ref):
    spectra, span, width = out_ref.shape
    start = pl.multiple_of(place[0] * span, span)
    for b in range(spectra):
        total = parts_ref[0, b].astype(F32)
        for part in range(1, NZ):
            total = total + parts_ref[part, b].astype(F32)
        rows = lax.broadcasted_iota(jnp.int32, (span, width), 0) + start
        mask = (rows < lengths[b]).astype(F32)
        own = x_ref[b, pl.ds(start, span)].astype(F32) * mask
        out_ref[b] = ((own + rows_ref[1:2] * total) * mask).astype(BF)


def close(place, lengths, parts, inputs, rows):
    _, spectra, span, width = parts.shape
    out = jax.ShapeDtypeStruct((spectra, span, width), BF)
    return pl.pallas_call(
        close_kernel,
        in_specs=[smem(), smem()] + [whole(a.shape) for a in (parts, inputs, rows)],
        out_specs=whole(out.shape),
        out_shape=out,
        cost_estimate=cost(2),
        name="close",
    )(place, lengths, parts, inputs, rows)


def swap_cores(value):
    return lax.ppermute(value, "c", [(0, 1), (1, 0)])


def order_matrix(width, share):
    slot = jnp.arange(NC * PLANE * BLOCK, dtype=jnp.int32)
    row = slot % BLOCK
    plane = (slot // BLOCK) % PLANE
    core = (slot // (BLOCK * PLANE) + lax.axis_index("c")) % NC
    natural = jnp.where(row < share, (plane * NC + core) * share + row, -1)
    return (natural[:, None] == jnp.arange(width, dtype=jnp.int32)[None, :]).astype(BF)


def step(inputs, cotangent, lengths, kernel, norm_gain, layer_scale, w_in, w_out):
    spectra, seq_len, width = inputs.shape
    units = w_in.shape[1]
    share = w_in.shape[0]
    tokens = spectra * seq_len
    span = seq_len // NZ
    half = PLANE * BLOCK
    blocks = (NZ, spectra, span, width)
    place = lax.axis_index("mp").astype(jnp.int32).reshape(1)
    rows = jnp.stack((norm_gain, layer_scale))
    flip = (((1,), (1,)), ((), ()))
    firsts = (((0,), (0,)), ((), ()))

    both = jnp.pad(jnp.concatenate((w_in, w_out.T), 1), ((0, BLOCK - share), (0, 0)))
    both = lax.all_to_all(jnp.broadcast_to(both[None], (PLANE, BLOCK, 2 * units)), ("x", "y"), 0, 0)
    order = order_matrix(width, share)
    normed, scaled, upstream, unit_own, inv_own, window = front(place, lengths, inputs, cotangent, kernel, rows)
    both, normed, order = lax.optimization_barrier((both, normed, order))
    normed = normed.reshape(tokens, width)
    scaled = scaled.reshape(tokens, width)
    both = both.reshape(half, 2 * units)
    arranged = jnp.concatenate((both, swap_cores(both)), 0)
    full = lax.dot_general(order, arranged, firsts, preferred_element_type=F32).astype(BF)
    full_in, full_out = full[:, :units], full[:, units:]

    hidden = jnp.dot(normed, full_in, preferred_element_type=F32)
    act_grad = jnp.dot(scaled, full_out, preferred_element_type=F32)
    hidden_grad = (act_grad * gelu_slope(hidden)).astype(BF)
    active = jax.nn.gelu(hidden, approximate=False).astype(BF)
    back_part = lax.dot_general(hidden_grad, full_in, flip, preferred_element_type=F32).astype(BF)
    back_part, hidden_grad, active = lax.optimization_barrier((back_part, hidden_grad, active))
    back_parts = lax.all_to_all(back_part.reshape(blocks), "mp", 0, 0)

    mixed_part = lax.dot_general(active, full_out, flip, preferred_element_type=F32).astype(BF)
    in_term = lax.dot_general(normed, hidden_grad, firsts, preferred_element_type=F32).astype(BF)
    out_term = lax.dot_general(scaled, active, firsts, preferred_element_type=F32).astype(BF)
    terms = jnp.concatenate((in_term, out_term), 1)
    far = jnp.dot(order[half:], terms, preferred_element_type=F32).astype(BF)
    near = jnp.dot(order[:half], terms, preferred_element_type=F32).astype(BF)
    terms = (near.astype(F32) + swap_cores(far).astype(F32)).astype(BF)
    scale_sum = jnp.sum(upstream.reshape(tokens, width).astype(F32) * mixed_part.astype(F32), 0)[None, :]
    back_parts, mixed_part, terms, scale_sum = lax.optimization_barrier((back_parts, mixed_part, terms, scale_sum))
    mixed_parts = lax.all_to_all(mixed_part.reshape(blocks), "mp", 0, 0)

    conv_grad, first, last, gain_sum = norm_back(back_parts, unit_own, inv_own, rows)
    before = lax.ppermute(last, "mp", [(i, i + 1) for i in range(NZ - 1)])
    after = lax.ppermute(first, "mp", [(i + 1, i) for i in range(NZ - 1)])
    terms = pack(conv_grad, window, gain_sum, scale_sum, order, terms).reshape(PLANE, BLOCK, -1)
    own_grad = conv_back(place, lengths, before, conv_grad, after, cotangent, kernel)

    terms, own_grad, mixed_parts = lax.optimization_barrier((terms, own_grad, mixed_parts))
    terms = lax.all_to_all(terms, ("x", "y"), 0, 0)
    blocks = lax.all_gather(own_grad, "mp", axis=0, tiled=False)

    terms = jnp.sum(terms.astype(F32), 0)

    near, far = terms[:, width : width + LANES], terms[:, width + LANES :]
    first_core = lax.axis_index("c") == 0
    small = jnp.stack((jnp.where(first_core, near, far), jnp.where(first_core, far, near)))
    small = jnp.broadcast_to(small[:, None], (NC, NZ, BLOCK, LANES)).reshape(NC * NZ, BLOCK, LANES)
    terms, blocks, mixed_parts, small = lax.optimization_barrier((terms, blocks, mixed_parts, small))
    input_grad = jnp.swapaxes(blocks, 0, 1).reshape(spectra, seq_len, width)
    output = close(place, lengths, mixed_parts, inputs, rows)
    grads = terms[:share, :width]
    small = lax.all_to_all(small, ("c", "mp"), 0, 0)
    small = jnp.sum(small, 0)[:share, : TAPS + 2].T
    return (
        output,
        input_grad,
        grads[:, :units],
        grads[:, units:].T,
        small[:TAPS],
        small[TAPS],
        small[TAPS + 1],
    )


def solution(mesh):
    fine = Mesh(mesh.devices.reshape(NX, NY, NC, NZ), ("x", "y", "c", "mp"))
    dp = ("x", "y", "c")
    placed = (
        P(dp, None, None),
        P(dp, None, None),
        P(dp),
        P(),
        P(),
        P(),
        P(dp, "mp"),
        P("mp", dp),
    )
    return jax.shard_map(
        step,
        mesh=fine,
        in_specs=placed,
        out_specs=(
            P(dp, "mp", None),
            P(dp, None, None),
            P(dp, "mp"),
            P("mp", dp),
            P(None, dp),
            P(dp),
            P(dp),
        ),
        check_vma=False,
    )
```

```python
import jax
import jax.numpy as jnp
from jax import lax
from jax.experimental import pallas as pl
from jax.experimental.pallas import tpu as pltpu
from jax.sharding import Mesh, PartitionSpec as P


NX, NY, NC, NZ = 8, 8, 2, 8
PLANE = NX * NY
LANES = 128
TAPS = 31
PAD = 16
BLOCK = 8
BF = jnp.bfloat16
F32 = jnp.float32


def gelu_slope(hidden):
    normal_cdf = 0.5 * (1.0 + jax.scipy.special.erf(hidden * 0.7071067811865476))
    density = jnp.exp(-0.5 * hidden * hidden) * 0.3989422804014327
    return normal_cdf + hidden * density


def whole(shape):
    return pl.BlockSpec(shape, lambda *_: (0,) * len(shape), memory_space=pltpu.VMEM)


def cost(micros):
    moved = int(micros * 3.0e6)
    return pl.CostEstimate(flops=0, transcendentals=0, bytes_accessed=moved)


def smem():
    return pl.BlockSpec(memory_space=pltpu.SMEM)


def shifted_sum(source, taps_of, weights, first, rows, temp):
    total = jnp.zeros((rows, LANES), F32)
    for residue in range(8):
        mine = [(s, tap) for s, tap in taps_of if s % 8 == residue]
        if residue:
            depth = max(s // 8 for s, _ in mine) * 8 + rows
            temp[residue - 1, :depth] = source(first + residue, depth)
        for s, tap in mine:
            at = s - residue
            moved = temp[residue - 1, at : at + rows] if residue else source(first + at, rows)
            total = total + weights(tap) * moved
    return total


def front_kernel(place, lengths, x_ref, cot_ref, taps_ref, rows_ref, normed_ref, scaled_ref, up_ref, unit_ref, inv_ref, win_ref, pad_ref, conv_ref, std_ref, temp_ref):
    spectra, seq_len, width = x_ref.shape
    span = seq_len // NZ
    z = place[0]
    edge = jnp.zeros((PAD, width), F32)

    def spectrum(b, _):
        length = lengths[b]
        pad_ref[:PAD] = edge
        pad_ref[PAD + seq_len :] = edge

        def fill(i, _):
            at = pl.multiple_of(i * span, span)
            rows = lax.broadcasted_iota(jnp.int32, (span, width), 0) + at
            mask = (rows < length).astype(F32)
            pad_ref[pl.ds(at + PAD, span)] = x_ref[b, pl.ds(at, span)].astype(F32) * mask
            up = cot_ref[b, pl.ds(at, span)].astype(F32) * mask
            scaled_ref[i, b] = (rows_ref[1:2] * up).astype(BF)
            up_ref[i, b] = up.astype(BF)
            return 0

        lax.fori_loop(0, NZ, fill, 0)
        win_ref[b] = pad_ref[pl.ds(pl.multiple_of(z * span, span), 2 * span)].astype(BF)

        def columns(j, _):
            lanes = pl.ds(pl.multiple_of(j * LANES, LANES), LANES)
            half = seq_len // 2
            for h in range(2):
                conv_ref[h * half : (h + 1) * half, lanes] = shifted_sum(
                    lambda start, depth: pad_ref[start : start + depth, lanes],
                    [(tap + 1, tap) for tap in range(TAPS)],
                    lambda tap: taps_ref[tap : tap + 1, lanes],
                    h * half,
                    half,
                    temp_ref.at[h],
                )
            return 0

        lax.fori_loop(0, width // LANES, columns, 0)

        def norm(i, _):
            at = pl.multiple_of(i * span, span)
            conv = conv_ref[pl.ds(at, span)]
            centred = conv - jnp.mean(conv, -1, keepdims=True)
            inv_std = lax.rsqrt(jnp.mean(centred * centred, -1, keepdims=True) + 1e-06)
            unit = centred * inv_std
            conv_ref[pl.ds(at, span)] = unit
            std_ref[pl.ds(at, span)] = jnp.broadcast_to(inv_std, (span, LANES))
            normed_ref[i, b] = (unit * rows_ref[:1]).astype(BF)
            return 0

        lax.fori_loop(0, NZ, norm, 0)
        own = pl.ds(pl.multiple_of(z * span, span), span)
        unit_ref[b] = conv_ref[own]
        inv_ref[b] = std_ref[own]
        return 0

    lax.fori_loop(0, spectra, spectrum, 0)


def front(place, lengths, inputs, cotangent, kernel, rows):
    spectra, seq_len, width = inputs.shape
    span = seq_len // NZ
    blocks = (NZ, spectra, span, width)
    outs = (
        jax.ShapeDtypeStruct(blocks, BF),
        jax.ShapeDtypeStruct(blocks, BF),
        jax.ShapeDtypeStruct(blocks, BF),
        jax.ShapeDtypeStruct((spectra, span, width), F32),
        jax.ShapeDtypeStruct((spectra, span, LANES), F32),
        jax.ShapeDtypeStruct((spectra, 2 * span, width), BF),
    )
    return pl.pallas_call(
        front_kernel,
        in_specs=[smem(), smem()] + [whole(a.shape) for a in (inputs, cotangent, kernel, rows)],
        out_specs=tuple(whole(o.shape) for o in outs),
        out_shape=outs,
        scratch_shapes=[
            pltpu.VMEM((seq_len + 2 * PAD, width), F32),
            pltpu.VMEM((seq_len, width), F32),
            pltpu.VMEM((seq_len, LANES), F32),
            pltpu.VMEM((2, 7, seq_len // 2 + 2 * PAD, LANES), F32),
        ],
        cost_estimate=cost(16),
        name="front",
    )(place, lengths, inputs, cotangent, kernel, rows)


def norm_back_kernel(parts_ref, unit_ref, inv_ref, rows_ref, grad_ref, first_ref, last_ref, gain_ref):
    spectra, span, width = unit_ref.shape
    gain_sum = jnp.zeros((1, width), F32)
    for b in range(spectra):
        total = parts_ref[0, b].astype(F32)
        for part in range(1, NZ):
            total = total + parts_ref[part, b].astype(F32)
        unit = unit_ref[b]
        gain_sum = gain_sum + jnp.sum(total * unit, 0, keepdims=True)
        g = total * rows_ref[:1]
        grad = inv_ref[b][:, :1] * (g - jnp.mean(g, -1, keepdims=True) - unit * jnp.mean(g * unit, -1, keepdims=True))
        grad_ref[b] = grad
        first_ref[b] = grad[:PAD].astype(BF)
        last_ref[b] = grad[span - PAD :].astype(BF)
    gain_ref[...] = gain_sum


def norm_back(parts, unit, inv, rows):
    spectra, span, width = unit.shape
    outs = (
        jax.ShapeDtypeStruct((spectra, span, width), F32),
        jax.ShapeDtypeStruct((spectra, PAD, width), BF),
        jax.ShapeDtypeStruct((spectra, PAD, width), BF),
        jax.ShapeDtypeStruct((1, width), F32),
    )
    return pl.pallas_call(
        norm_back_kernel,
        in_specs=[whole(a.shape) for a in (parts, unit, inv, rows)],
        out_specs=tuple(whole(o.shape) for o in outs),
        out_shape=outs,
        cost_estimate=cost(2),
        compiler_params=pltpu.CompilerParams(vmem_limit_bytes=10 << 20),
        name="norm_back",
    )(parts, unit, inv, rows)


def taps_kernel(grad_ref, win_ref, gain_ref, scale_ref, order_ref, near_ref, far_ref, win_f, sums_ref, temp_ref):
    spectra, span, width = grad_ref.shape
    half = near_ref.shape[0]
    for b in range(spectra):
        win_f[b] = win_ref[b].astype(F32)
    sums_ref[...] = jnp.zeros(sums_ref.shape, F32)
    sums_ref[TAPS : TAPS + 1] = gain_ref[...]
    sums_ref[TAPS + 1 : TAPS + 2] = scale_ref[...]

    def columns(j, _):
        lanes = pl.ds(pl.multiple_of(j * LANES, LANES), LANES)
        grads = [grad_ref[b, :, lanes] for b in range(spectra)]
        for residue in range(8):
            depth = 2 * span - 8
            for b in range(spectra):
                temp_ref[b, residue] = win_f[b, residue : residue + depth, lanes]
            for s in range(residue, TAPS + 1, 8):
                if s:
                    at = s - residue
                    product = grads[0] * temp_ref[0, residue, at : at + span]
                    for b in range(1, spectra):
                        product = product + grads[b] * temp_ref[b, residue, at : at + span]
                    sums_ref[s - 1 : s, lanes] = jnp.sum(product, 0, keepdims=True)
        return 0

    lax.fori_loop(0, width // LANES, columns, 0)
    sums = sums_ref[...].astype(BF)
    for core, out_ref in enumerate((near_ref, far_ref)):
        turned = lax.dot_general(
            order_ref[core * half : (core + 1) * half], sums, (((1,), (1,)), ((), ())), preferred_element_type=F32
        )
        out_ref[...] = turned.astype(BF)


def tap_sums(grad, window, gain_sum, scale_sum, order):
    spectra, span, width = grad.shape
    out = jax.ShapeDtypeStruct((order.shape[0] // NC, LANES), BF)
    return pl.pallas_call(
        taps_kernel,
        in_specs=[whole(a.shape) for a in (grad, window, gain_sum, scale_sum, order)],
        out_specs=(whole(out.shape),) * NC,
        out_shape=(out,) * NC,
        scratch_shapes=[
            pltpu.VMEM((spectra, 2 * span, width), F32),
            pltpu.VMEM((LANES, width), F32),
            pltpu.VMEM((spectra, 8, 2 * span - 8, LANES), F32),
        ],
        cost_estimate=cost(3),
        compiler_params=pltpu.CompilerParams(vmem_limit_bytes=10 << 20),
        name="tap_sums",
    )(grad, window, gain_sum, scale_sum, order)


def conv_back_kernel(place, lengths, before_ref, grad_ref, after_ref, cot_ref, taps_ref, out_ref, ext_ref, temp_ref):
    spectra, span, width = grad_ref.shape
    start = pl.multiple_of(place[0] * span, span)
    for b in range(spectra):
        ext_ref[b, :PAD] = before_ref[b].astype(F32)
        ext_ref[b, PAD : PAD + span] = grad_ref[b]
        ext_ref[b, PAD + span :] = after_ref[b].astype(F32)

    def columns(j, _):
        lanes = pl.ds(pl.multiple_of(j * LANES, LANES), LANES)
        for b in range(spectra):
            total = shifted_sum(
                lambda first, depth: ext_ref[b, first : first + depth, lanes],
                [(TAPS - tap, tap) for tap in range(TAPS)],
                lambda tap: taps_ref[tap : tap + 1, lanes],
                0,
                span,
                temp_ref.at[b],
            )
            rows = lax.broadcasted_iota(jnp.int32, (span, LANES), 0) + start
            mask = (rows < lengths[b]).astype(F32)
            up = cot_ref[b, pl.ds(start, span), lanes].astype(F32) * mask
            out_ref[b, :, lanes] = ((up + total) * mask).astype(BF)
        return 0

    lax.fori_loop(0, width // LANES, columns, 0)


def conv_back(place, lengths, before, grad, after, cotangent, kernel):
    spectra, span, width = grad.shape
    out = jax.ShapeDtypeStruct((spectra, span, width), BF)
    return pl.pallas_call(
        conv_back_kernel,
        in_specs=[smem(), smem()] + [whole(a.shape) for a in (before, grad, after, cotangent, kernel)],
        out_specs=whole(out.shape),
        out_shape=out,
        scratch_shapes=[
            pltpu.VMEM((spectra, span + 2 * PAD, width), F32),
            pltpu.VMEM((spectra, 7, span + 2 * PAD, LANES), F32),
        ],
        cost_estimate=cost(3),
        compiler_params=pltpu.CompilerParams(vmem_limit_bytes=10 << 20),
        name="conv_back",
    )(place, lengths, before, grad, after, cotangent, kernel)


def close_kernel(place, lengths, parts_ref, x_ref, rows_ref, out_ref):
    spectra, span, width = out_ref.shape
    start = pl.multiple_of(place[0] * span, span)
    for b in range(spectra):
        total = parts_ref[0, b].astype(F32)
        for part in range(1, NZ):
            total = total + parts_ref[part, b].astype(F32)
        rows = lax.broadcasted_iota(jnp.int32, (span, width), 0) + start
        mask = (rows < lengths[b]).astype(F32)
        own = x_ref[b, pl.ds(start, span)].astype(F32) * mask
        out_ref[b] = ((own + rows_ref[1:2] * total) * mask).astype(BF)


def close(place, lengths, parts, inputs, rows):
    _, spectra, span, width = parts.shape
    out = jax.ShapeDtypeStruct((spectra, span, width), BF)
    return pl.pallas_call(
        close_kernel,
        in_specs=[smem(), smem()] + [whole(a.shape) for a in (parts, inputs, rows)],
        out_specs=whole(out.shape),
        out_shape=out,
        cost_estimate=cost(2),
        compiler_params=pltpu.CompilerParams(vmem_limit_bytes=10 << 20),
        name="close",
    )(place, lengths, parts, inputs, rows)


def swap_cores(value):
    return lax.ppermute(value, "c", [(0, 1), (1, 0)])


def order_matrix(width, share, block):
    slot = jnp.arange(NC * PLANE * block, dtype=jnp.int32)
    row = slot % block
    plane = (slot // block) % PLANE
    core = (slot // (block * PLANE) + lax.axis_index("c")) % NC
    natural = jnp.where(row < share, (plane * NC + core) * share + row, -1)
    return (natural[:, None] == jnp.arange(width, dtype=jnp.int32)[None, :]).astype(BF)


def step(inputs, cotangent, lengths, kernel, norm_gain, layer_scale, w_in, w_out):
    spectra, seq_len, width = inputs.shape
    units = w_in.shape[1]
    share = w_in.shape[0]
    tokens = spectra * seq_len
    span = seq_len // NZ
    half = PLANE * BLOCK
    blocks = (NZ, spectra, span, width)
    place = lax.axis_index("mp").astype(jnp.int32).reshape(1)
    rows = jnp.stack((norm_gain, layer_scale))
    flip = (((1,), (1,)), ((), ()))
    firsts = (((0,), (0,)), ((), ()))

    both = jnp.concatenate((w_in, w_out.T), 1).reshape(share // 2, 2, 2 * units)
    both = lax.all_to_all(jnp.broadcast_to(both[None], (PLANE,) + both.shape), ("x", "y"), 0, 0)
    order = order_matrix(width, share, BLOCK)
    normed, scaled, upstream, unit_own, inv_own, window = front(place, lengths, inputs, cotangent, kernel, rows)
    both, normed, order = lax.optimization_barrier((both, normed, order))
    normed = normed.reshape(tokens, width)
    scaled = scaled.reshape(tokens, width)
    other = swap_cores(both).reshape(PLANE * share, 2 * units)
    both = both.reshape(PLANE * share, 2 * units)
    arranged = jnp.concatenate((both, other), 0)
    natural = order_matrix(width, share, share)
    full = lax.dot_general(natural, arranged, firsts, preferred_element_type=F32).astype(BF)
    full_in, full_out = full[:, :units], full[:, units:]

    hidden = jnp.dot(normed, full_in, preferred_element_type=F32)
    act_grad = jnp.dot(scaled, full_out, preferred_element_type=F32)
    hidden_grad = (act_grad * gelu_slope(hidden)).astype(BF)
    back_part = lax.dot_general(hidden_grad, full_in, flip, preferred_element_type=F32).astype(BF)
    back_part, hidden_grad, hidden = lax.optimization_barrier((back_part, hidden_grad, hidden))
    back_parts = lax.all_to_all(back_part.reshape(blocks), "mp", 0, 0)

    active = jax.nn.gelu(hidden, approximate=False).astype(BF)
    mixed_part = lax.dot_general(active, full_out, flip, preferred_element_type=F32).astype(BF)
    in_term = lax.dot_general(normed, hidden_grad, firsts, preferred_element_type=F32).astype(BF)
    out_term = lax.dot_general(scaled, active, firsts, preferred_element_type=F32).astype(BF)
    terms = jnp.concatenate((in_term, out_term), 1)
    far = jnp.dot(order[half:], terms, preferred_element_type=F32).astype(BF)
    near = jnp.dot(order[:half], terms, preferred_element_type=F32).astype(BF)
    terms = (near.astype(F32) + swap_cores(far).astype(F32)).astype(BF)
    scale_sum = jnp.sum(upstream.reshape(tokens, width).astype(F32) * mixed_part.astype(F32), 0)[None, :]
    back_parts, mixed_part, terms, scale_sum = lax.optimization_barrier((back_parts, mixed_part, terms, scale_sum))
    mixed_parts = lax.all_to_all(mixed_part.reshape(blocks), "mp", 0, 0)

    conv_grad, first, last, gain_sum = norm_back(back_parts, unit_own, inv_own, rows)
    before = lax.ppermute(last, "mp", [(i, i + 1) for i in range(NZ - 1)])
    after = lax.ppermute(first, "mp", [(i + 1, i) for i in range(NZ - 1)])
    near, far = tap_sums(conv_grad, window, gain_sum, scale_sum, order)
    small = (near.astype(F32) + swap_cores(far).astype(F32)).astype(BF)
    terms = jnp.concatenate((terms, small), 1).reshape(PLANE, BLOCK, -1)
    own_grad = conv_back(place, lengths, before, conv_grad, after, cotangent, kernel)

    terms, own_grad, mixed_parts = lax.optimization_barrier((terms, own_grad, mixed_parts))
    terms = lax.all_to_all(terms, ("x", "y"), 0, 0)
    blocks = lax.all_gather(own_grad, "mp", axis=0, tiled=False)

    terms = jnp.sum(terms.astype(F32), 0)

    small = jnp.broadcast_to(terms[None, :, width:], (NZ, BLOCK, LANES))
    terms, blocks, mixed_parts, small = lax.optimization_barrier((terms, blocks, mixed_parts, small))
    input_grad = jnp.swapaxes(blocks, 0, 1).reshape(spectra, seq_len, width)
    output = close(place, lengths, mixed_parts, inputs, rows)
    grads = terms[:share, :width]
    small = lax.all_to_all(small, "mp", 0, 0)
    small = jnp.sum(small, 0)[:share, : TAPS + 2].T
    return (
        output,
        input_grad,
        grads[:, :units],
        grads[:, units:].T,
        small[:TAPS],
        small[TAPS],
        small[TAPS + 1],
    )


def solution(mesh):
    fine = Mesh(mesh.devices.reshape(NX, NY, NC, NZ), ("x", "y", "c", "mp"))
    dp = ("x", "y", "c")
    placed = (
        P(dp, None, None),
        P(dp, None, None),
        P(dp),
        P(),
        P(),
        P(),
        P(dp, "mp"),
        P("mp", dp),
    )
    return jax.shard_map(
        step,
        mesh=fine,
        in_specs=placed,
        out_specs=(
            P(dp, "mp", None),
            P(dp, None, None),
            P(dp, "mp"),
            P("mp", dp),
            P(None, dp),
            P(dp),
            P(dp),
        ),
        check_vma=False,
    )
```
